128 devices in a mesh: seq: 8 (over y, core), nbr: 16 (over z, x).
Axes of the slice: x: 4, y: 4, z: 4, core: 2. Of those that a mesh axis runs over, the one named last changes fastest.
Arguments:
- queries: bfloat16 [32768, 2048], P(('seq', 'nbr')), may hold values from -16 to 16
- cotangent: bfloat16 [32768, 2048], P(('seq', 'nbr')), may hold values from -6 to 6
- neighbour_tokens: bfloat16 [1024, 128, 896], P(('seq', 'nbr')), may hold values from -6 to 6
- neighbour_ids: int32 [512, 2], P(('seq', 'nbr')), may hold values from 0 to 1023, as said below
- neighbour_dest: int32 [1024], P(('seq', 'nbr')), may hold values from 0 to 1023, as said below
- sequence_ids: int32 [512], P(('seq', 'nbr')), may hold values from 0 to 31, never falling along the last dimension, each value on 1 to 32 neighbouring positions
- enc_in: bfloat16 [896, 1792], replicated, may hold values from -0.1875 to 0.1875
- enc_out: bfloat16 [1792, 896], replicated, may hold values from -0.125 to 0.125
- key_weight: bfloat16 [896, 2048], replicated, may hold values from -0.5 to 0.5
- value_weight: bfloat16 [896, 2048], replicated, may hold values from -0.1875 to 0.1875
Outputs:
- attended: bfloat16 [32768, 2048], P(('seq', 'nbr'))
- grad_encoded: bfloat16 [1024, 128, 896], P(('seq', 'nbr'))
The draws below stay inside these ranges and needn't reach their ends.
Inputs may be any that keep to these rules, and one draw needn't show every extreme that they name: `neighbour_ids`: every number 0 to 1023 appears exactly once. Neighbour n is held by device n // 8 in the order seq+nbr, a device of the same seq index as the device holding the span. Among the neighbours of one device's spans at most 2 are held by any one device, and in every draw some device has exactly 2 held by one device. neighbour_dest[neighbour_ids[c, k]] = c * 2 + k for every span c and k.
All inputs are finite; a program needn't handle non-finite values.
Results may differ from the reference program's by a relative error of at most 0.015.
The reference program's roundings to bfloat16 on the way count: a program that leaves them out, or rounds other values in their place, can miss the bound.
Values may be sent and summed in bfloat16 or wider, within the bound.
No kernel may reach another device: no remote copies, remote signals or barrier semaphores. Data moves between devices by JAX's collectives and lax.ppermute only.
A program may use at most 128 MiB of HBM per device.

```python
import math
import jax
import jax.numpy as jnp
import numpy as np
from jax import lax

ENC = 896
HEAD_DIM = 128
HEADS = 16
ENC_FF = 1792
SPAN = 64
NEIGH_LEN = 128
TOPK = 2
CH_DEV = 4
NB_DEV = 8
SPANS = 512
TOKENS = 32768
NEIGHBOURS = 1024
N_SEQ = 8
N_NBR = 16
DEVICES = 128


def one_group(group_key, group_idx):
    peer_count = N_NBR
    half_slots = NB_DEV // 2
    slot_total = peer_count * NB_DEV
    subkeys = jax.random.split(group_key, 6)
    first_set = jax.random.permutation(subkeys[0], peer_count)[:half_slots]
    relabel = jax.random.permutation(subkeys[1], peer_count)
    source = jax.random.randint(subkeys[2], (), 0, peer_count)
    target = (source + first_set[0]) % peer_count
    wanted = (relabel[target] - relabel[source]) % peer_count
    shuffled = jax.random.permutation(subkeys[3], peer_count)
    position = jnp.argmax(shuffled == wanted)
    swapped = shuffled.at[position].set(shuffled[0]).at[0].set(wanted)
    second = swapped[:half_slots]
    inverse = jnp.argsort(relabel)
    row_index = jnp.arange(peer_count)
    owners_a = (row_index[:, None] + first_set[None, :]) % peer_count
    owners_b = inverse[(relabel[:, None] + second[None, :]) % peer_count]
    owners = jnp.concatenate([owners_a, owners_b], axis=1)
    row_keys = jax.random.split(subkeys[4], peer_count)
    shuffle = jax.vmap(lambda row_key: jax.random.permutation(row_key, NB_DEV))(row_keys)
    owners = jnp.take_along_axis(owners, shuffle, axis=1).reshape(-1)
    scores = owners * slot_total + jax.random.permutation(subkeys[5], slot_total)
    placing = jnp.argsort(jnp.argsort(scores))
    local_idx = placing - owners * NB_DEV
    return ((group_idx * peer_count + owners) * NB_DEV + local_idx).astype(jnp.int32)


def routing(key):
    group_keys = jax.random.split(jax.random.fold_in(key, 7), N_SEQ)
    grouped = jax.vmap(one_group)(group_keys, jnp.arange(N_SEQ))
    return grouped.reshape(-1).astype(jnp.int32)


def draw_neighbour_ids(key, part):
    return routing(key).reshape(SPANS, TOPK)


def draw_neighbour_dest(key, part):
    return jnp.argsort(routing(key)).astype(jnp.int32)


def draw_queries(key, part):
    base_key = jax.random.fold_in(jax.random.fold_in(key, 11), 0)
    base_draw = jax.random.truncated_normal(base_key, -6.0, 6.0, (TOKENS, HEADS * HEAD_DIM), jnp.float32)
    return base_draw.astype(jnp.bfloat16)


def level_of(rng, extent, cuts, least, top_value):
    def one(axis_at, parts):
        draws = jax.random.uniform(jax.random.fold_in(jax.random.fold_in(rng, 6), axis_at), (parts,), jnp.float32, least / len(cuts), top_value / len(cuts))
        return jnp.repeat(jnp.exp(draws), extent[axis_at] // parts).reshape((-1,) + (1,) * (len(extent) - axis_at - 1))

    level = one(*cuts[0])
    for cut in cuts[1:]:
        level = level * one(*cut)
    return level


def length_profile(amount, total, most, skew):
    portions = [(1 << 20) // math.isqrt(grade ** skew) + 1 for grade in range(2, amount + 1)]
    rest, counts = total - most - (amount - 1), [1] * (amount - 1)
    while rest > 0:
        free = [i for i in range(amount - 1) if counts[i] < most]
        pool, budget = sum([portions[i] for i in free]), rest
        for i in free:
            extra = min(most - counts[i], max(1, budget * portions[i] // pool), rest)
            counts[i] = counts[i] + extra
            rest = rest - extra
    return np.array([most] + counts)


def uneven(stream_key, count, total, most, slope):
    if count == 2:
        one = jax.random.randint(stream_key, (), max(1, total - most), min(most, total - 1) + 1)
        return jnp.stack([one, total - one])
    lengths = jnp.asarray(length_profile(count, total, most, slope), jnp.int32)
    twos = (count - 1) // 2
    giver, receiver = lengths[1:1 + 2 * twos:2], lengths[2:2 + 2 * twos:2]
    room = jnp.minimum(giver - 1, most - receiver)
    moved = jax.random.randint(jax.random.fold_in(stream_key, 1), (twos,), 0, 1 << 20) % (room + 1)
    lengths = lengths.at[1:1 + 2 * twos:2].set(giver - moved).at[2:2 + 2 * twos:2].set(receiver + moved)
    return lengths[jax.random.permutation(jax.random.fold_in(stream_key, 2), count)]


def scatter_about(stream_key, dims, width, limit, shards=(), held_as=jnp.bfloat16):
    values = jax.random.normal(stream_key, dims, jnp.float32) * width
    if len(shards) > 0:
        values = level_of(stream_key, dims, shards, -0.22, 0.18) * values
    return jnp.clip(values, min=-limit, max=limit).astype(held_as)


def setup_inputs(seed: int = 0) -> dict:
    keys = jax.random.split(jax.random.key(seed), 11)
    return {
        "queries": draw_queries(jax.random.fold_in(keys[10], 71), 0),
        "cotangent": scatter_about(keys[1], (TOKENS, HEADS * HEAD_DIM), 1.0, 6.0, ((0, 128),)),
        "neighbour_tokens": scatter_about(keys[2], (NEIGHBOURS, NEIGH_LEN, ENC), 1.0, 6.0, ((0, 128),)),
        "neighbour_ids": draw_neighbour_ids(jax.random.fold_in(keys[10], 71), 0),
        "neighbour_dest": draw_neighbour_dest(jax.random.fold_in(keys[10], 71), 0),
        "sequence_ids": jnp.searchsorted(jnp.cumsum(uneven(keys[5], SPANS // 16, SPANS, 32, 2)), jnp.arange(SPANS), side="right").astype(jnp.int32),
        "enc_in": scatter_about(keys[6], (ENC, ENC_FF), ENC ** -0.5, 0.1875),
        "enc_out": scatter_about(keys[7], (ENC_FF, ENC), ENC_FF ** -0.5, 0.125),
        "key_weight": scatter_about(keys[8], (ENC, HEADS * HEAD_DIM), (ENC // 8) ** -0.5, 0.5),
        "value_weight": scatter_about(keys[9], (ENC, HEADS * HEAD_DIM), ENC ** -0.5, 0.1875),
    }


epsilon = 1e-06

def as_float(values_in):
    return lax.optimization_barrier(values_in).astype(jnp.float32)

def encode(block, enc_in, enc_out):
    inputs = block.astype(jnp.float32)
    scaling = lax.rsqrt(lax.optimization_barrier(jnp.mean(inputs * inputs, axis=-1, keepdims=True)) + epsilon)
    normed = (inputs * scaling).astype(jnp.bfloat16)
    hidden_act = jax.nn.gelu(jnp.dot(normed, enc_in, preferred_element_type=jnp.float32), approximate=True).astype(jnp.bfloat16)
    return (inputs + jnp.dot(hidden_act, enc_out, preferred_element_type=jnp.float32)).astype(jnp.bfloat16)

def attend(query_rows, cot_rows, slot_block, validity, key_weight, value_weight):
    blocks, span_len, features = query_rows.shape
    head_count = features // HEAD_DIM
    slot_count, length, enc_width = slot_block.shape
    flat_slots = slot_block.reshape(slot_count * length, enc_width)
    key_rows = jnp.dot(flat_slots, key_weight, preferred_element_type=jnp.float32).astype(jnp.bfloat16)
    value_rows = jnp.dot(flat_slots, value_weight, preferred_element_type=jnp.float32).astype(jnp.bfloat16)
    key_rows = as_float(key_rows).reshape(blocks, -1, head_count, HEAD_DIM)
    value_rows = as_float(value_rows).reshape(blocks, -1, head_count, HEAD_DIM)
    query_four = query_rows.astype(jnp.float32).reshape(blocks, span_len, head_count, HEAD_DIM)
    inv_root = 1.0 / math.sqrt(HEAD_DIM)
    scores = jnp.einsum('cmhd,cphd->chmp', query_four, key_rows) * inv_root
    shares = jax.nn.softmax(scores, axis=-1)
    weights = as_float(shares.astype(jnp.bfloat16))
    mixture = jnp.einsum('chmp,cphd->cmhd', weights, value_rows)
    attended = (mixture * validity[:, :, None, None]).astype(jnp.bfloat16).reshape(blocks, span_len, features)
    masked = cot_rows.astype(jnp.float32).reshape(blocks, span_len, head_count, HEAD_DIM) * validity[:, :, None, None]
    grad_weights = jnp.einsum('cmhd,cphd->chmp', masked, value_rows)
    grad_scores = shares * (grad_weights - lax.optimization_barrier(jnp.sum(shares * grad_weights, axis=-1, keepdims=True)))
    grad_scores = as_float(grad_scores.astype(jnp.bfloat16))
    grad_keys = (jnp.einsum('chmp,cmhd->cphd', grad_scores, query_four) * inv_root).astype(jnp.bfloat16)
    grad_values = jnp.einsum('chmp,cmhd->cphd', weights, masked).astype(jnp.bfloat16)
    grad_keys = grad_keys.reshape(slot_count * length, features)
    grad_values = grad_values.reshape(slot_count * length, features)
    slot_grads = jnp.dot(grad_keys, key_weight.T, preferred_element_type=jnp.float32) + jnp.dot(grad_values, value_weight.T, preferred_element_type=jnp.float32)
    return (attended, slot_grads.astype(jnp.bfloat16).reshape(slot_count, length, enc_width))

def reference(queries, cotangent, neighbour_tokens, neighbour_ids, neighbour_dest, sequence_ids, enc_in, enc_out, key_weight, value_weight):
    length = neighbour_tokens.shape[1]
    enc_width = neighbour_tokens.shape[2]
    features = queries.shape[1]
    blocks_in = neighbour_tokens.reshape(DEVICES, NB_DEV * length, enc_width)
    encoded = lax.map(lambda block: encode(block, enc_in, enc_out), blocks_in).reshape(NEIGHBOURS, length, enc_width)
    head_rows = SPAN - 1
    pad_rows = jnp.zeros((head_rows, features), queries.dtype)
    query_ext = jnp.concatenate([queries[head_rows:], pad_rows], 0).reshape(DEVICES, CH_DEV, SPAN, features)
    cot_ext = jnp.concatenate([cotangent[head_rows:], pad_rows], 0).reshape(DEVICES, CH_DEV, SPAN, features)
    later_ids = jnp.concatenate([sequence_ids[1:], jnp.full((1,), -1, jnp.int32)], 0)
    offsets = jnp.arange(SPAN)
    validity = ((offsets[None, :] == 0) | (sequence_ids[:, None] == later_ids[:, None])).astype(jnp.float32)
    validity = validity.reshape(DEVICES, CH_DEV, SPAN)
    slot_ids = neighbour_ids.reshape(DEVICES, NB_DEV).astype(jnp.int32)

    def one_block(inputs):
        query_rows, cot_rows, valid_rows, indices = inputs
        slot_block = jnp.take(encoded, indices, axis=0)
        return attend(query_rows, cot_rows, slot_block, valid_rows, key_weight, value_weight)
    attended_ext, slot_grads = lax.map(one_block, (query_ext, cot_ext, validity, slot_ids))
    attended_ext = attended_ext.reshape(TOKENS, features)
    attended = jnp.concatenate([pad_rows, attended_ext[:TOKENS - head_rows]], 0)
    grad_encoded = jnp.take(slot_grads.reshape(SPANS * TOPK, length, enc_width), neighbour_dest.astype(jnp.int32), axis=0)
    return (attended, grad_encoded)
```

```python
import math

import jax
import jax.numpy as jnp
from jax import lax
from jax.experimental import pallas as pl
from jax.experimental.pallas import tpu as pltpu
from jax.sharding import PartitionSpec as P

HEAD = 128
EPS = 1e-06
PIECE = 8
NT = (((1,), (1,)), ((), ()))
TN = (((0,), (0,)), ((), ()))
F32 = jnp.float32
BF16 = jnp.bfloat16
VMEM_LIMIT = 56 * 1024 * 1024


def params(n=1):
    return pltpu.CompilerParams(
        dimension_semantics=("arbitrary",) * n, vmem_limit_bytes=VMEM_LIMIT
    )


def from_behind(block, axis, distance):
    devices = range(lax.axis_size(axis))
    route = [(i - distance, i) for i in devices if i - distance in devices]
    return lax.ppermute(block, axis, route)


def spread(block):
    return lax.all_to_all(block, "nbr", split_axis=0, concat_axis=0, tiled=True)


def encode_kernel(tok_ref, ids_ref, win_ref, wout_ref, out_ref, normed, acc):
    step = pl.program_id(0)
    count, length, width = tok_ref.shape
    pieces = length // PIECE

    @pl.when(step == 0)
    def _():
        for i in range(count):
            x = tok_ref[i].astype(F32)
            scale = lax.rsqrt(jnp.mean(x * x, axis=-1, keepdims=True) + EPS)
            normed[pl.ds(i * length, length), :] = (x * scale).astype(BF16)
            acc[pl.ds(i * length, length), :] = x

    rows = 256
    for b in range(count * length // rows):
        at = pl.ds(b * rows, rows)
        hidden = jnp.dot(normed[at, :], win_ref[...], preferred_element_type=F32)
        hidden = jax.nn.gelu(hidden, approximate=True).astype(BF16)
        acc[at, :] += jnp.dot(hidden, wout_ref[...], preferred_element_type=F32)

    @pl.when(step == pl.num_programs(0) - 1)
    def _():
        for i in range(count):
            y = acc[pl.ds(i * length, length), :].astype(BF16)
            out_ref[:, i] = y.reshape(pieces, PIECE, width)
        for p in range(pieces):
            out_ref[p, count] = ids_ref[...]


def encode(tokens, ids, enc_in, enc_out):
    count, length, width = tokens.shape
    hidden = enc_in.shape[1]
    block = 256
    pieces = length // PIECE
    return pl.pallas_call(
        encode_kernel,
        grid=(hidden // block,),
        in_specs=[
            pl.BlockSpec((count, length, width), lambda f: (0, 0, 0)),
            pl.BlockSpec((PIECE, width), lambda f: (0, 0)),
            pl.BlockSpec((width, block), lambda f: (0, f)),
            pl.BlockSpec((block, width), lambda f: (f, 0)),
        ],
        out_specs=pl.BlockSpec((pieces, count + 1, PIECE, width), lambda f: (0, 0, 0, 0)),
        out_shape=jax.ShapeDtypeStruct((pieces, count + 1, PIECE, width), BF16),
        scratch_shapes=[
            pltpu.VMEM((count * length, width), BF16),
            pltpu.VMEM((count * length, width), F32),
        ],
        compiler_params=params(),
        name="encode",
    )(tokens, ids, enc_in, enc_out)


def reorder_kernel(inverse, table_ref, src_ref, dst_ref, sem):
    peers, count = dst_ref.shape[:2]

    def body(k, carry):
        at = table_ref[k]
        there = (at // count, at % count)
        here = (k // count, k % count)
        a, b = (here, there) if inverse else (there, here)
        pltpu.make_async_copy(src_ref.at[a[0], a[1]], dst_ref.at[b[0], b[1]], sem).start()
        return carry

    lax.fori_loop(0, peers * count, body, 0, unroll=8)
    pltpu.make_async_copy(src_ref.at[:, :count], dst_ref, sem).wait()


def reorder(table, block, count, inverse):
    return pl.pallas_call(
        lambda *refs: reorder_kernel(inverse, *refs),
        grid_spec=pltpu.PrefetchScalarGridSpec(
            num_scalar_prefetch=1,
            in_specs=[pl.BlockSpec(memory_space=pltpu.VMEM)],
            out_specs=pl.BlockSpec(memory_space=pl.ANY),
            scratch_shapes=[pltpu.SemaphoreType.DMA],
        ),
        out_shape=jax.ShapeDtypeStruct(block.shape[:1] + (count,) + block.shape[2:], block.dtype),
        compiler_params=pltpu.CompilerParams(vmem_limit_bytes=VMEM_LIMIT),
        name="reorder_back" if inverse else "reorder",
    )(table, block)


def regroup_kernel(src_ref, dst_ref, sem):
    copies = [
        pltpu.make_async_copy(src_ref.at[:, i], dst_ref.at[i], sem.at[i])
        for i in range(dst_ref.shape[0])
    ]
    for copy in copies:
        copy.start()
    for copy in copies:
        copy.wait()


def regroup(block):
    pieces, count, rows, width = block.shape
    out = pl.pallas_call(
        regroup_kernel,
        in_specs=[pl.BlockSpec(memory_space=pltpu.VMEM)],
        out_specs=pl.BlockSpec(memory_space=pl.ANY),
        out_shape=jax.ShapeDtypeStruct((count, pieces, rows, width), block.dtype),
        scratch_shapes=[pltpu.SemaphoreType.DMA((count,))],
        name="regroup",
    )(block)
    return out.reshape(count, pieces * rows, width)


def span_rows(own, later, span):
    last = lax.broadcasted_iota(jnp.int32, (span, own.shape[1]), 0) == span - 1
    blocks = own.shape[0] // span
    out = []
    for c in range(blocks):
        here = own[c * span : (c + 1) * span]
        after = own[(c + 1) * span : (c + 2) * span] if c + 1 < blocks else later
        out.append(jnp.where(last, here, after))
    return out


def row_valid(valid_ref, c, span, width):
    last = lax.broadcasted_iota(jnp.int32, (span, width), 0) == span - 1
    return jnp.where(last, 1.0, valid_ref[c].astype(F32))


def project_kernel(valid_ref, q_ref, nq_ref, g_ref, ng_ref, wk_ref, wv_ref, qw_ref, mw_ref):
    spans, heads, span, width = qw_ref.shape
    inv_root = 1.0 / math.sqrt(HEAD)
    q = span_rows(q_ref[...].astype(F32), nq_ref[...].astype(F32), span)
    g = span_rows(g_ref[...].astype(F32), ng_ref[...].astype(F32), span)
    g = [g[c] * row_valid(valid_ref, c, span, g[c].shape[1]) for c in range(spans)]
    q = jnp.concatenate(q, 0).astype(BF16)
    g = jnp.concatenate(g, 0).astype(BF16)
    for h in range(heads):
        at = slice(h * HEAD, (h + 1) * HEAD)
        qw = lax.dot_general(q[:, at], wk_ref[:, at], NT, preferred_element_type=F32)
        qw_ref[:, h] = (qw * inv_root).astype(BF16).reshape(spans, span, width)
        mw = lax.dot_general(g[:, at], wv_ref[:, at], NT, preferred_element_type=F32)
        mw_ref[:, h] = mw.astype(BF16).reshape(spans, span, width)


def project(valid, queries, next_query, cotangent, next_cot, key_weight, value_weight, span):
    rows, features = queries.shape
    width = key_weight.shape[0]
    spans = rows // span
    heads = 2
    block = heads * HEAD
    tall = pl.BlockSpec((rows, block), lambda f, v: (0, f))
    short = pl.BlockSpec((span, block), lambda f, v: (0, f))
    wide = pl.BlockSpec((width, block), lambda f, v: (0, f))
    out = pl.BlockSpec((spans, heads, span, width), lambda f, v: (0, f, 0, 0))
    shape = jax.ShapeDtypeStruct((spans, features // HEAD, span, width), BF16)
    return pl.pallas_call(
        project_kernel,
        grid_spec=pltpu.PrefetchScalarGridSpec(
            num_scalar_prefetch=1,
            grid=(features // block,),
            in_specs=[tall, short, tall, short, wide, wide],
            out_specs=[out, out],
        ),
        out_shape=[shape, shape],
        compiler_params=params(),
        name="project",
    )(valid, queries, next_query, cotangent, next_cot, key_weight, value_weight)


def attend_kernel(x_ref, qw_ref, mw_ref, grad_ref, weight_ref):
    pieces, _, rows, width = x_ref.shape
    x = x_ref[:, 0].reshape(pieces * rows, width)
    columns = qw_ref.shape[1]
    block = 256
    total = None
    for b in range(columns // block):
        at = slice(b * block, (b + 1) * block)
        qw = qw_ref[0, at, :]
        mw = mw_ref[0, at, :]
        scores = lax.dot_general(x, qw, NT, preferred_element_type=F32)
        grad_weights = lax.dot_general(x, mw, NT, preferred_element_type=F32)
        shares = jnp.exp(scores - jnp.max(scores, axis=0, keepdims=True))
        shares = shares * (1.0 / jnp.sum(shares, axis=0, keepdims=True))
        weights = shares.astype(BF16)
        inner = jnp.sum(shares * grad_weights, axis=0, keepdims=True)
        grad_scores = (shares * (grad_weights - inner)).astype(BF16)
        weight_ref[0, :, at] = weights
        part = jnp.dot(grad_scores, qw, preferred_element_type=F32) + jnp.dot(
            weights, mw, preferred_element_type=F32
        )
        total = part if total is None else total + part
    grad_ref[:, 0] = total.astype(BF16).reshape(pieces, rows, width)


def attend(slots, qw, mw):
    pieces, spans, rows, width = slots.shape
    columns = qw.shape[1]
    piece = pl.BlockSpec((pieces, 1, rows, width), lambda c: (0, c, 0, 0))
    projected = pl.BlockSpec((1, columns, width), lambda c: (c, 0, 0))
    return pl.pallas_call(
        attend_kernel,
        grid=(spans,),
        in_specs=[piece, projected, projected],
        out_specs=[piece, pl.BlockSpec((1, pieces * rows, columns), lambda c: (c, 0, 0))],
        out_shape=[
            jax.ShapeDtypeStruct(slots.shape, BF16),
            jax.ShapeDtypeStruct((spans, pieces * rows, columns), BF16),
        ],
        compiler_params=params(),
        name="attend",
    )(slots, qw, mw)


def mix_kernel(valid_ref, x_ref, weight_ref, wv_ref, out_ref, tail_ref, before):
    c = pl.program_id(0)
    pieces, _, rows, width = x_ref.shape
    span = out_ref.shape[0]
    x = x_ref[:, 0].reshape(pieces * rows, width)
    pair = 2 * HEAD
    scale = row_valid(valid_ref, c, span, HEAD)
    last = lax.broadcasted_iota(jnp.int32, (span, HEAD), 0) == span - 1
    for b in range(wv_ref.shape[1] // pair):
        values = jnp.dot(x, wv_ref[:, b * pair : (b + 1) * pair], preferred_element_type=F32)
        weights = weight_ref[0, :, b * 2 * span : (b + 1) * 2 * span]
        mixed = lax.dot_general(weights, values.astype(BF16), TN, preferred_element_type=F32)
        for h in range(2):
            at = slice(b * pair + h * HEAD, b * pair + (h + 1) * HEAD)
            now = mixed[h * span : (h + 1) * span, h * HEAD : (h + 1) * HEAD] * scale
            out_ref[:, at] = jnp.where(last, now, before[:, at]).astype(BF16)
            before[:, at] = now

    @pl.when(c == pl.num_programs(0) - 1)
    def _():
        tail_ref[...] = before[...].astype(BF16)


def mix(valid, slots, weights, value_weight, span):
    pieces, spans, rows, width = slots.shape
    features = value_weight.shape[1]
    return pl.pallas_call(
        mix_kernel,
        grid_spec=pltpu.PrefetchScalarGridSpec(
            num_scalar_prefetch=1,
            grid=(spans,),
            in_specs=[
                pl.BlockSpec((pieces, 1, rows, width), lambda c, v: (0, c, 0, 0)),
                pl.BlockSpec((1,) + weights.shape[1:], lambda c, v: (c, 0, 0)),
                pl.BlockSpec((width, features), lambda c, v: (0, 0)),
            ],
            out_specs=[
                pl.BlockSpec((span, features), lambda c, v: (c, 0)),
                pl.BlockSpec((span, features), lambda c, v: (0, 0)),
            ],
            scratch_shapes=[pltpu.VMEM((span, features), F32)],
        ),
        out_shape=[
            jax.ShapeDtypeStruct((spans * span, features), BF16),
            jax.ShapeDtypeStruct((span, features), BF16),
        ],
        compiler_params=params(),
        name="mix",
    )(valid, slots, weights, value_weight)


def join_kernel(whole_ref, carried_ref, out_ref):
    span, features = out_ref.shape
    last = lax.broadcasted_iota(jnp.int32, (span, features), 0) == span - 1
    out_ref[...] = jnp.where(
        last, whole_ref[...].astype(F32), carried_ref[...].astype(F32)
    ).astype(BF16)


def join(whole, carried):
    first = pl.BlockSpec(carried.shape, lambda i: (0, 0))
    return pl.pallas_call(
        join_kernel,
        grid=(1,),
        in_specs=[first, first],
        out_specs=first,
        out_shape=jax.ShapeDtypeStruct(whole.shape, whole.dtype),
        input_output_aliases={0: 0},
        compiler_params=params(),
        name="join",
    )(whole, carried)


def shards(
    queries,
    cotangent,
    neighbour_tokens,
    neighbour_ids,
    neighbour_dest,
    sequence_ids,
    enc_in,
    enc_out,
    key_weight,
    value_weight,
):
    spans = sequence_ids.shape[0]
    rows, features = queries.shape
    span = rows // spans
    count, length, width = neighbour_tokens.shape
    peers = lax.axis_size("nbr")
    everyone = ("seq", "nbr")

    own_ids = (neighbour_ids.reshape(1, count) % (peers * count)).astype(BF16)
    own_ids = jnp.pad(own_ids, ((0, PIECE - 1), (0, width - count)))
    next_label = from_behind(sequence_ids[:1] + 1, everyone, -1)
    next_query = from_behind(queries[:span], everyone, -1)
    next_cot = from_behind(cotangent[:span], everyone, -1)
    labels = sequence_ids + 1
    valid = (labels == jnp.concatenate([labels[1:], next_label], 0)).astype(jnp.int32)

    pieces = encode(neighbour_tokens, own_ids, enc_in, enc_out)
    pieces, next_query, next_cot, valid = lax.optimization_barrier(
        (pieces, next_query, next_cot, valid)
    )
    held = spread(pieces)
    table = held[:, count, 0, :count].astype(jnp.int32).reshape(-1)
    qw, mw = project(
        valid, queries, next_query, cotangent, next_cot, key_weight, value_weight, span
    )
    held, table, qw, mw = lax.optimization_barrier((held, table, qw, mw))
    slots = spread(reorder(table, held, count, False))
    pair = (peers, spans, count // spans * PIECE, width)
    columns = features // HEAD * span
    grads, weights = attend(
        slots.reshape(pair), qw.reshape(spans, columns, width), mw.reshape(spans, columns, width)
    )
    held_grads = spread(grads.reshape(slots.shape))
    whole, tail = mix(valid, slots.reshape(pair), weights, value_weight, span)
    carried = from_behind(tail, everyone, 1)
    attended = join(whole, carried)
    returned = spread(reorder(table, held_grads, count, True))
    return attended, regroup(returned)


def solution(mesh):
    rows = P(("seq", "nbr"), None)
    blocks = P(("seq", "nbr"), None, None)
    flat = P(("seq", "nbr"))
    in_specs = (rows, rows, blocks, rows, flat, flat, P(), P(), P(), P())
    return jax.shard_map(
        shards, mesh=mesh, in_specs=in_specs, out_specs=(rows, blocks), check_vma=False
    )
```

```python
import math

import jax
import jax.numpy as jnp
from jax import lax
from jax.experimental import pallas as pl
from jax.experimental.pallas import tpu as pltpu
from jax.sharding import PartitionSpec as P

HEAD = 128
EPS = 1e-06
PIECE = 8
NT = (((1,), (1,)), ((), ()))
TN = (((0,), (0,)), ((), ()))
F32 = jnp.float32
BF16 = jnp.bfloat16
VMEM_LIMIT = 32 * 1024 * 1024


def params(n=1):
    return pltpu.CompilerParams(
        dimension_semantics=("arbitrary",) * n, vmem_limit_bytes=VMEM_LIMIT
    )


def from_behind(block, axis, distance):
    devices = range(lax.axis_size(axis))
    route = [(i - distance, i) for i in devices if i - distance in devices]
    return lax.ppermute(block, axis, route)


def spread(block):
    return lax.all_to_all(block, "nbr", split_axis=0, concat_axis=0, tiled=True)


def in_vmem(block):
    return pltpu.with_memory_space_constraint(block, pltpu.VMEM)


def in_hbm(block):
    return pltpu.with_memory_space_constraint(block, pltpu.HBM)


def encode_kernel(ids_ref, tok, win, wout_hbm, out_ref, wout, normed, hid, stage, sems):
    count, length, width = tok.shape
    pieces = length // PIECE
    items = count // 2
    rows = items * length
    chunk = 256
    wout_copy = pltpu.make_async_copy(wout_hbm, wout, sems.at[0])
    wout_copy.start()

    row = lax.broadcasted_iota(jnp.int32, (PIECE, width), 0)
    own = jnp.zeros((PIECE, width), jnp.int32)
    for r in range(count):
        own = jnp.where(row == r, ids_ref[r % 2, r // 2] % (pieces * count), own)
    own = own.astype(F32).astype(BF16)
    for p in range(pieces):
        stage[p, count] = own

    def norm(b):
        x = tok[pl.ds(b * items, items)].reshape(rows, width).astype(F32)
        scale = lax.rsqrt(jnp.mean(x * x, axis=-1, keepdims=True) + EPS)
        normed[b] = (x * scale).astype(BF16)

    outs = []
    norm(0)
    for b in range(2):
        for f in range(win.shape[1] // chunk):
            at = slice(f * chunk, (f + 1) * chunk)
            hidden = jnp.dot(normed[b], win[:, at], preferred_element_type=F32)
            hid[b, :, at] = jax.nn.gelu(hidden, approximate=True).astype(BF16)
        if b == 0:
            norm(1)
            wout_copy.wait()
        y = jnp.dot(hid[b], wout[...], preferred_element_type=F32)
        y = (y + tok[pl.ds(b * items, items)].reshape(rows, width).astype(F32)).astype(BF16)
        for i in range(items):
            stage[:, b * items + i] = y[i * length : (i + 1) * length].reshape(pieces, PIECE, width)
        part = pl.ds(b * items, items + b)
        outs.append(pltpu.make_async_copy(stage.at[:, part], out_ref.at[:, part], sems.at[1 + b]))
        outs[b].start()
    for copy in outs:
        copy.wait()


def encode(tokens, ids, enc_in, enc_out):
    count, length, width = tokens.shape
    hidden = enc_in.shape[1]
    shape = (length // PIECE, count + 1, PIECE, width)
    rows = count // 2 * length
    inside = pl.BlockSpec(memory_space=pltpu.VMEM)
    anywhere = pl.BlockSpec(memory_space=pltpu.HBM)
    return pl.pallas_call(
        encode_kernel,
        in_specs=[pl.BlockSpec(memory_space=pltpu.SMEM), inside, inside, anywhere],
        out_specs=anywhere,
        out_shape=pltpu.HBM(shape, BF16),
        scratch_shapes=[
            pltpu.VMEM(enc_out.shape, BF16),
            pltpu.VMEM((2, rows, width), BF16),
            pltpu.VMEM((2, rows, hidden), BF16),
            pltpu.VMEM(shape, BF16),
            pltpu.SemaphoreType.DMA((3,)),
        ],
        compiler_params=pltpu.CompilerParams(vmem_limit_bytes=32 << 20),
        name="encode",
    )(ids.T, in_vmem(tokens), in_vmem(enc_in), in_hbm(enc_out))


def reorder_kernel(inverse, table_ref, src_ref, dst_ref, sem):
    peers, count = dst_ref.shape[:2]
    for j in range(peers):
        for k in range(count):
            at = table_ref[j * count + k]
            there = (at // count, at % count)
            a, b = ((j, k), there) if inverse else (there, (j, k))
            pltpu.make_async_copy(src_ref.at[a[0], a[1]], dst_ref.at[b[0], b[1]], sem).start()
    pltpu.make_async_copy(src_ref.at[:, pl.ds(0, count)], dst_ref, sem).wait()


def reorder(table, block, count, inverse):
    return pl.pallas_call(
        lambda *refs: reorder_kernel(inverse, *refs),
        grid_spec=pltpu.PrefetchScalarGridSpec(
            num_scalar_prefetch=1,
            in_specs=[pl.BlockSpec(memory_space=pltpu.VMEM)],
            out_specs=pl.BlockSpec(memory_space=pltpu.HBM),
            scratch_shapes=[pltpu.SemaphoreType.DMA],
        ),
        out_shape=pltpu.HBM(block.shape[:1] + (count,) + block.shape[2:], block.dtype),
        compiler_params=pltpu.CompilerParams(vmem_limit_bytes=4 << 20),
        name="reorder_back" if inverse else "reorder",
    )(table, in_vmem(block))


def regroup_kernel(src_ref, dst_ref, sem):
    copies = [
        pltpu.make_async_copy(src_ref.at[:, i], dst_ref.at[i], sem.at[i])
        for i in range(dst_ref.shape[0])
    ]
    for copy in copies:
        copy.start()
    for copy in copies:
        copy.wait()


def regroup(block):
    pieces, count, rows, width = block.shape
    out = pl.pallas_call(
        regroup_kernel,
        in_specs=[pl.BlockSpec(memory_space=pltpu.VMEM)],
        out_specs=pl.BlockSpec(memory_space=pltpu.HBM),
        out_shape=jax.ShapeDtypeStruct((count, pieces, rows, width), block.dtype),
        scratch_shapes=[pltpu.SemaphoreType.DMA((count,))],
        compiler_params=pltpu.CompilerParams(vmem_limit_bytes=4 << 20),
        name="regroup",
    )(in_vmem(block))
    return out.reshape(count, pieces * rows, width)


def pack_kernel(label_ref, q_ref, g_ref, tok_hbm, win_hbm, out_ref, tok_ref, win_ref, q, g, sems):
    span = q.shape[0]
    copies = [
        pltpu.make_async_copy(q_ref.at[pl.ds(0, span)], q, sems.at[0]),
        pltpu.make_async_copy(g_ref.at[pl.ds(0, span)], g, sems.at[1]),
        pltpu.make_async_copy(tok_hbm, tok_ref, sems.at[2]),
        pltpu.make_async_copy(win_hbm, win_ref, sems.at[3]),
    ]
    for copy in copies:
        copy.start()
    for copy in copies[:2]:
        copy.wait()
    last = lax.broadcasted_iota(jnp.int32, q.shape, 0) == span - 1
    label = (label_ref[0] + 1).astype(F32)
    out_ref[0] = jnp.where(last, label, q[...].astype(F32)).astype(BF16)
    out_ref[1] = g[...]
    for copy in copies[2:]:
        copy.wait()


def pack(sequence_ids, queries, cotangent, tokens, enc_in, span):
    features = queries.shape[1]
    inside = pl.BlockSpec(memory_space=pltpu.VMEM)
    anywhere = pl.BlockSpec(memory_space=pltpu.HBM)
    return pl.pallas_call(
        pack_kernel,
        in_specs=[pl.BlockSpec(memory_space=pltpu.SMEM)] + [anywhere] * 4,
        out_specs=[inside] * 3,
        out_shape=[
            pltpu.VMEM((2, span, features), BF16),
            pltpu.VMEM(tokens.shape, BF16),
            pltpu.VMEM(enc_in.shape, BF16),
        ],
        scratch_shapes=[
            pltpu.VMEM((span, features), BF16),
            pltpu.VMEM((span, features), BF16),
            pltpu.SemaphoreType.DMA((4,)),
        ],
        compiler_params=pltpu.CompilerParams(vmem_limit_bytes=16 << 20),
        name="pack",
    )(sequence_ids, in_hbm(queries), in_hbm(cotangent), in_hbm(tokens), in_hbm(enc_in))


def span_rows(own, later, span):
    last = lax.broadcasted_iota(jnp.int32, (span, own.shape[1]), 0) == span - 1
    blocks = own.shape[0] // span
    out = []
    for c in range(blocks):
        here = own[c * span : (c + 1) * span]
        after = own[(c + 1) * span : (c + 2) * span] if c + 1 < blocks else later
        out.append(jnp.where(last, here, after))
    return out


def row_valid(valid_ref, c, span, width):
    last = lax.broadcasted_iota(jnp.int32, (span, width), 0) == span - 1
    return jnp.where(last, 1.0, valid_ref[c].astype(F32))


def project_kernel(valid_ref, q_ref, g_ref, next_ref, wk_ref, wv_ref, out_ref):
    spans, _, heads, span, width = out_ref.shape
    inv_root = 1.0 / math.sqrt(HEAD)
    q = span_rows(q_ref[...].astype(F32), next_ref[0].astype(F32), span)
    g = span_rows(g_ref[...].astype(F32), next_ref[1].astype(F32), span)
    g = [g[c] * row_valid(valid_ref, c, span, g[c].shape[1]) for c in range(spans)]
    q = jnp.concatenate(q, 0).astype(BF16)
    g = jnp.concatenate(g, 0).astype(BF16)
    for h in range(heads):
        at = slice(h * HEAD, (h + 1) * HEAD)
        qw = lax.dot_general(q[:, at], wk_ref[:, at], NT, preferred_element_type=F32)
        out_ref[:, 0, h] = (qw * inv_root).astype(BF16).reshape(spans, span, width)
        mw = lax.dot_general(g[:, at], wv_ref[:, at], NT, preferred_element_type=F32)
        out_ref[:, 1, h] = mw.astype(BF16).reshape(spans, span, width)


def project(valid, queries, cotangent, next_rows, key_weight, value_weight, span):
    rows, features = queries.shape
    width = key_weight.shape[0]
    spans = rows // span
    heads = 2
    block = heads * HEAD
    tall = pl.BlockSpec((rows, block), lambda f, v: (0, f))
    short = pl.BlockSpec((2, span, block), lambda f, v: (0, 0, f))
    wide = pl.BlockSpec((width, block), lambda f, v: (0, f))
    out = pl.BlockSpec((spans, 2, heads, span, width), lambda f, v: (0, 0, f, 0, 0))
    shape = pltpu.HBM((spans, 2, features // HEAD, span, width), BF16)
    return pl.pallas_call(
        project_kernel,
        grid_spec=pltpu.PrefetchScalarGridSpec(
            num_scalar_prefetch=1,
            grid=(features // block,),
            in_specs=[tall, tall, short, wide, wide],
            out_specs=out,
        ),
        out_shape=shape,
        compiler_params=pltpu.CompilerParams(
            dimension_semantics=("arbitrary",), vmem_limit_bytes=16 << 20
        ),
        name="project",
    )(valid, queries, cotangent, next_rows, key_weight, value_weight)


def attend_kernel(
    x_ref, proj_hbm, grad_ref, weight_ref, proj_ref, shares_out, grads_out, scored, sems, proj_sems
):
    pieces, spans, rows, width = x_ref.shape
    columns = proj_ref.shape[2]
    block = 256

    def arrival(c, b):
        at = pl.ds(b * columns // 2, columns // 2)
        return pltpu.make_async_copy(
            proj_hbm.at[c, :, at], proj_ref.at[c, :, at], proj_sems.at[c, b]
        )

    arrival(0, 0).start()
    arrival(0, 1).start()

    def span(c):
        x = x_ref[:, c].reshape(pieces * rows, width)

        def products(b):
            if b == 0:
                arrival(c, 0).wait()
                if c + 1 < spans:
                    arrival(c + 1, 0).start()
                    arrival(c + 1, 1).start()
                if c > 0:
                    arrival(c, 1).wait()
            if c == 0 and b == columns // block // 2:
                arrival(0, 1).wait()
            at = slice(b * block, (b + 1) * block)
            return (
                lax.dot_general(x, proj_ref[c, 0, at, :], NT, preferred_element_type=F32),
                lax.dot_general(x, proj_ref[c, 1, at, :], NT, preferred_element_type=F32),
            )

        later = products(0)
        for b in range(columns // block):
            scores, grad_weights = later
            if (b + 1) * block < columns:
                later = products(b + 1)
            at = slice(b * block, (b + 1) * block)
            shares = jnp.exp(scores - jnp.max(scores, axis=0, keepdims=True))
            shares = shares * (1.0 / jnp.sum(shares, axis=0, keepdims=True))
            inner = jnp.sum(shares * grad_weights, axis=0, keepdims=True)
            shares_out[c, :, at] = shares.astype(BF16)
            scored[c % 2, :, at] = (shares * (grad_weights - inner)).astype(BF16)

    copies = []

    def finish(c):
        total = jnp.dot(scored[c % 2], proj_ref[c, 0], preferred_element_type=F32)
        total += jnp.dot(shares_out[c], proj_ref[c, 1], preferred_element_type=F32)
        grads_out[c] = total.astype(BF16).reshape(pieces, rows, width)
        copies.append(pltpu.make_async_copy(grads_out.at[c], grad_ref.at[:, c], sems.at[0, c]))
        copies[-1].start()

    for c in range(spans + 1):
        if c < spans:
            span(c)
            copies.append(pltpu.make_async_copy(shares_out.at[c], weight_ref.at[c], sems.at[1, c]))
            copies[-1].start()
        if c > 0:
            finish(c - 1)
    for copy in copies:
        copy.wait()


def attend(slots, projected):
    pieces, spans, rows, width = slots.shape
    columns = projected.shape[2]
    shares = (spans, pieces * rows, columns)
    inside = pl.BlockSpec(memory_space=pltpu.VMEM)
    anywhere = pl.BlockSpec(memory_space=pltpu.HBM)
    return pl.pallas_call(
        attend_kernel,
        in_specs=[inside, anywhere],
        out_specs=[anywhere] * 2,
        out_shape=[pltpu.HBM(slots.shape, BF16), pltpu.HBM(shares, BF16)],
        scratch_shapes=[
            pltpu.VMEM(projected.shape, BF16),
            pltpu.VMEM(shares, BF16),
            pltpu.VMEM((spans, pieces, rows, width), BF16),
            pltpu.VMEM((2,) + shares[1:], BF16),
            pltpu.SemaphoreType.DMA((2, spans)),
            pltpu.SemaphoreType.DMA((spans, 2)),
        ],
        compiler_params=pltpu.CompilerParams(vmem_limit_bytes=40 << 20),
        name="attend",
    )(in_vmem(slots), in_hbm(projected))


def mix_kernel(valid_ref, x_ref, weight_ref, wv_ref, out_ref, tail_ref, before):
    c = pl.program_id(0)
    pieces, _, rows, width = x_ref.shape
    span = out_ref.shape[0]
    x = x_ref[:, 0].reshape(pieces * rows, width)
    pair = 2 * HEAD
    scale = row_valid(valid_ref, c, span, HEAD)
    last = lax.broadcasted_iota(jnp.int32, (span, HEAD), 0) == span - 1
    for b in range(wv_ref.shape[1] // pair):
        values = jnp.dot(x, wv_ref[:, b * pair : (b + 1) * pair], preferred_element_type=F32)
        weights = weight_ref[0, :, b * 2 * span : (b + 1) * 2 * span]
        mixed = lax.dot_general(weights, values.astype(BF16), TN, preferred_element_type=F32)
        for h in range(2):
            at = slice(b * pair + h * HEAD, b * pair + (h + 1) * HEAD)
            now = mixed[h * span : (h + 1) * span, h * HEAD : (h + 1) * HEAD] * scale
            out_ref[:, at] = jnp.where(last, now, before[:, at]).astype(BF16)
            before[:, at] = now

    @pl.when(c == pl.num_programs(0) - 1)
    def _():
        tail_ref[...] = before[...].astype(BF16)


def mix(valid, slots, weights, value_weight, span):
    pieces, spans, rows, width = slots.shape
    features = value_weight.shape[1]
    return pl.pallas_call(
        mix_kernel,
        grid_spec=pltpu.PrefetchScalarGridSpec(
            num_scalar_prefetch=1,
            grid=(spans,),
            in_specs=[
                pl.BlockSpec((pieces, 1, rows, width), lambda c, v: (0, c, 0, 0)),
                pl.BlockSpec((1,) + weights.shape[1:], lambda c, v: (c, 0, 0)),
                pl.BlockSpec((width, features), lambda c, v: (0, 0)),
            ],
            out_specs=[
                pl.BlockSpec((span, features), lambda c, v: (c, 0)),
                pl.BlockSpec((span, features), lambda c, v: (0, 0)),
            ],
            scratch_shapes=[pltpu.VMEM((span, features), F32)],
        ),
        out_shape=[
            jax.ShapeDtypeStruct((spans * span, features), BF16),
            jax.ShapeDtypeStruct((span, features), BF16),
        ],
        compiler_params=params(),
        name="mix",
    )(valid, slots, weights, value_weight)


def join_kernel(whole_ref, carried_ref, out_ref):
    span, features = out_ref.shape
    last = lax.broadcasted_iota(jnp.int32, (span, features), 0) == span - 1
    out_ref[...] = jnp.where(
        last, whole_ref[...].astype(F32), carried_ref[...].astype(F32)
    ).astype(BF16)


def join(whole, carried):
    first = pl.BlockSpec(carried.shape, lambda i: (0, 0))
    return pl.pallas_call(
        join_kernel,
        grid=(1,),
        in_specs=[first, first],
        out_specs=first,
        out_shape=jax.ShapeDtypeStruct(whole.shape, whole.dtype),
        input_output_aliases={0: 0},
        compiler_params=params(),
        name="join",
    )(whole, carried)


def shards(
    queries,
    cotangent,
    neighbour_tokens,
    neighbour_ids,
    neighbour_dest,
    sequence_ids,
    enc_in,
    enc_out,
    key_weight,
    value_weight,
):
    spans = sequence_ids.shape[0]
    rows, features = queries.shape
    span = rows // spans
    count, length, width = neighbour_tokens.shape
    peers = lax.axis_size("nbr")
    everyone = ("seq", "nbr")

    first_rows, tokens, up = pack(
        sequence_ids, queries, cotangent, neighbour_tokens, enc_in, span
    )
    next_rows = from_behind(first_rows, everyone, -1)
    pieces = encode(tokens, neighbour_ids, up, enc_out)
    pieces, next_rows = lax.optimization_barrier((pieces, next_rows))
    held = spread(pieces)
    labels = (sequence_ids + 1).astype(BF16)
    next_label = next_rows[0, span - 1, :1]
    valid = (labels == jnp.concatenate([labels[1:], next_label], 0)).astype(jnp.int32)
    table = held[:, count, :, 0].astype(jnp.int32).reshape(-1)
    projected = project(valid, queries, cotangent, next_rows, key_weight, value_weight, span)
    held, table, projected = lax.optimization_barrier((held, table, projected))
    slots = spread(reorder(table, held, count, False))
    pair = (peers, spans, count // spans * PIECE, width)
    columns = features // HEAD * span
    grads, weights = attend(slots.reshape(pair), projected.reshape(spans, 2, columns, width))
    held_grads = spread(grads.reshape(slots.shape))
    whole, tail = mix(valid, slots.reshape(pair), weights, value_weight, span)
    held_grads, whole, tail = lax.optimization_barrier((held_grads, whole, tail))
    carried = from_behind(tail, everyone, 1)
    attended = join(whole, carried)
    returned = spread(reorder(table, held_grads, count, True))
    return attended, regroup(returned)


def solution(mesh):
    rows = P(("seq", "nbr"), None)
    blocks = P(("seq", "nbr"), None, None)
    flat = P(("seq", "nbr"))
    in_specs = (rows, rows, blocks, rows, flat, flat, P(), P(), P(), P())
    return jax.shard_map(
        shards, mesh=mesh, in_specs=in_specs, out_specs=(rows, blocks), check_vma=False
    )
```
